256 devices in a mesh: seq: 16 (over z, core), head: 8 (over x_lo, y), batch: 2 (over x_hi).
Axes of the slice: x: 4 (x_hi: 2, x_lo: 2; x = x_hi * 2 + x_lo), y: 4, z: 8, core: 2. Of those that a mesh axis runs over, the one named last changes fastest.
Arguments:
- queries: bfloat16 [8192, 4096], P(('batch', 'seq'), 'head'), parts along dimension 0, may hold values from -16 to 16, as said below
- key_rows: bfloat16 [8192, 1024], P(('batch', 'seq'), 'head'), parts along dimension 0, may hold values from -16 to 16
- value_rows: bfloat16 [8192, 1024], P(('batch', 'seq'), 'head'), parts along dimension 0, may hold values from -6 to 6
- out_grad: bfloat16 [8192, 4096], P(('batch', 'seq'), 'head'), parts along dimension 0, may hold values from -6 to 6
- tile_ids: int32 [64], P('batch'), parts along dimension 0, may hold values from 0 to 31, each once
- tile_mask: int32 [64, 32], P('batch'), parts along dimension 0, may hold values from 0 to 1, as said below
Outputs:
- attended: bfloat16 [8192, 4096], P(('batch', 'seq'), 'head'), parts along dimension 0
- query_grad: float32 [8192, 4096], P(('batch', 'seq'), 'head'), parts along dimension 0
- key_grad: float32 [8192, 1024], P(('batch', 'seq'), 'head'), parts along dimension 0
- value_grad: float32 [8192, 1024], P(('batch', 'seq'), 'head'), parts along dimension 0
The draws below stay inside these ranges and needn't reach their ends.
There are 2 independent parts, one for each index of `batch`. The reference program is written for one: setup_inputs(seed, part) draws one part's arguments, and reference() takes and returns one part's arrays. A program takes and returns all parts, laid end to end along the dimension named above; each array names one. Nothing has to cross between parts.
Inputs may be any that keep to these rules, and one draw needn't show every extreme that they name: `queries`: in the hidden draw a few query rows equal scaled key rows of the same tile. `tile_mask`: 1 only where the key tile's index is at most the query tile's; 1 on the diagonal.
All inputs are finite; a program needn't handle non-finite values.
Results may differ from the reference program's by a relative error of at most 0.03.
Values may be sent and summed in bfloat16 or wider, within the bound.
A program may use at most 64 MiB of HBM per device.

```python
import jax
import jax.numpy as jnp
from jax import lax

NH = 4
HD = 128
TILE = 128
KVH = 8
TOKENS = 4096
NT = 32


def draw_queries(key, part):
    base = jnp.clip(jax.random.normal(jax.random.fold_in(key, 1), (TOKENS, KVH * NH * HD), jnp.float32), -4.0, 4.0)
    return base.astype(jnp.bfloat16)


def draw_key_rows(key, part):
    base = jnp.clip(jax.random.normal(jax.random.fold_in(key, 2), (TOKENS, KVH * HD), jnp.float32), -4.0, 4.0)
    return base.astype(jnp.bfloat16)


def draw_tile_mask(key, part):
    tiles = TOKENS // TILE
    prompt = max(1, tiles // 8)
    answers = min(16, tiles - prompt)
    room = tiles - prompt - 1
    cuts = jnp.sort(jax.random.permutation(jax.random.fold_in(key, 5), room)[:answers - 1]).astype(jnp.int32)
    bounds = jnp.concatenate([jnp.array([-1], jnp.int32), cuts, jnp.array([room], jnp.int32)])
    lengths = bounds[1:] - bounds[:-1]
    ends = prompt + jnp.cumsum(lengths)
    places = jnp.arange(tiles, dtype=jnp.int32)
    segment = jnp.where(places < prompt, 0, 1 + jnp.sum((places[:, None] >= ends[None, :answers - 1]).astype(jnp.int32), axis=1))
    allowed = (places[None, :] <= places[:, None]) & ((segment[None, :] == 0) | (segment[None, :] == segment[:, None]))
    return allowed.astype(jnp.int32)


def level_of(stream_key, shape, split, least, top_value):
    def one(position, blocks):
        draws = jax.random.uniform(jax.random.fold_in(jax.random.fold_in(stream_key, 6), position), (blocks,), jnp.float32, least / len(split), top_value / len(split))
        return jnp.repeat(jnp.exp(draws), shape[position] // blocks).reshape((-1,) + (1,) * (len(shape) - position - 1))

    factor_of = one(*split[0])
    for cut in split[1:]:
        factor_of = factor_of * one(*cut)
    return factor_of


def scatter_about(key, dims, width, bound, pieces=(), kind=jnp.bfloat16):
    gain = level_of(key, dims, pieces, -0.22, 0.18) if pieces else 1.0
    entries = jax.random.normal(key, dims, jnp.float32) * width * gain
    return jnp.minimum(jnp.maximum(entries, -bound), bound).astype(kind)


def setup_inputs(seed: int = 0, part: int = 0) -> dict:
    key_of = jax.random.split(jax.random.key(seed), 7)
    part_splits = jax.random.split(jax.random.fold_in(key_of[6], part), 7)
    queries = draw_queries(jax.random.fold_in(jax.random.fold_in(key_of[6], part), 71), part)
    key_rows = draw_key_rows(jax.random.fold_in(jax.random.fold_in(key_of[6], part), 71), part)
    value_rows = scatter_about(part_splits[2], (TOKENS, KVH * HD), 1.0, 6.0, ((0, 16), (1, 8)))
    out_grad = scatter_about(part_splits[3], (TOKENS, KVH * NH * HD), 1.0, 6.0, ((0, 16), (1, 8)))
    tile_ids = jax.random.permutation(part_splits[4], NT).astype(jnp.int32)
    tile_mask = draw_tile_mask(jax.random.fold_in(jax.random.fold_in(key_of[6], part), 71), part)
    return dict(queries=queries, key_rows=key_rows, value_rows=value_rows, out_grad=out_grad, tile_ids=tile_ids, tile_mask=tile_mask)


far_below = -1.0e30


def rounded(values):
    return lax.optimization_barrier(values.astype(jnp.bfloat16)).astype(jnp.float32)


def tile_allowed(tile_mask, query_tiles, key_tiles):
    table = jnp.take(jnp.take(tile_mask, query_tiles, axis=0), key_tiles, axis=1) == 1
    same_tile = query_tiles[:, None] == key_tiles[None, :]
    inside = lax.broadcasted_iota(jnp.int32, (TILE, TILE), 0) >= lax.broadcasted_iota(jnp.int32, (TILE, TILE), 1)
    full = table[:, None, :, None] & (jnp.logical_not(same_tile)[:, None, :, None] | inside[None, :, None, :])
    return full.reshape(query_tiles.shape[0] * TILE, key_tiles.shape[0] * TILE)


def one_group(queries, key_rows, value_rows, out_grad, tile_ids, tile_mask):
    factor = HD ** -0.5
    block_rows = min(512, TOKENS)
    block_count = TOKENS // block_rows
    query_blocks = queries.reshape(block_count, block_rows, NH, HD)
    grad_blocks = out_grad.reshape(block_count, block_rows, NH, HD)
    tile_blocks = tile_ids.reshape(block_count, block_rows // TILE)
    keys_wide = key_rows.astype(jnp.float32)
    values_wide = value_rows.astype(jnp.float32)

    def scores_for(query_block, tile_block):
        allowed = tile_allowed(tile_mask, tile_block, tile_ids)[None]
        scores = jnp.einsum('qhd,kd->hqk', query_block.astype(jnp.float32), keys_wide) * factor
        return allowed, jnp.where(allowed, scores, far_below)

    def forward(inputs):
        query_block, tile_block = inputs
        allowed, scores = scores_for(query_block, tile_block)
        row_max = jnp.max(scores, axis=-1)
        softmax_terms = jnp.where(allowed, jnp.exp(scores - row_max[..., None]), 0.0)
        denominator = jnp.sum(softmax_terms, axis=-1)
        weighted = jnp.einsum('hqk,kd->qhd', rounded(softmax_terms), values_wide)
        output = (weighted / denominator.T[:, :, None]).astype(jnp.bfloat16)
        return output, row_max + jnp.log(denominator)

    outputs, log_totals = lax.map(forward, (query_blocks, tile_blocks))

    def backward(carry, inputs):
        key_sum, value_sum = carry
        query_block, out_block, grad_block, log_total, tile_block = inputs
        allowed, scores = scores_for(query_block, tile_block)
        softmax_terms = jnp.where(allowed, jnp.exp(scores - log_total[..., None]), 0.0)
        row_delta = jnp.sum(grad_block.astype(jnp.float32) * out_block.astype(jnp.float32), axis=-1).T
        dprobs = jnp.einsum('qhd,kd->hqk', grad_block.astype(jnp.float32), values_wide)
        dscores = rounded(softmax_terms * (dprobs - row_delta[..., None]))
        query_part = jnp.einsum('hqk,kd->qhd', dscores, keys_wide) * factor
        key_sum = key_sum + jnp.einsum('hqk,qhd->kd', dscores, query_block.astype(jnp.float32)) * factor
        value_sum = value_sum + jnp.einsum('hqk,qhd->kd', rounded(softmax_terms), grad_block.astype(jnp.float32))
        return (key_sum, value_sum), query_part

    zeros_wide = jnp.zeros((TOKENS, HD), jnp.float32)
    (key_grad, value_grad), query_parts = lax.scan(backward, (zeros_wide, zeros_wide), (query_blocks, outputs, grad_blocks, log_totals, tile_blocks))
    return outputs.reshape(TOKENS, NH, HD), query_parts.reshape(TOKENS, NH, HD), key_grad, value_grad


def reference(queries, key_rows, value_rows, out_grad, tile_ids, tile_mask):
    query_groups = jnp.transpose(queries.reshape(TOKENS, KVH, NH, HD), (1, 0, 2, 3))
    grad_groups = jnp.transpose(out_grad.reshape(TOKENS, KVH, NH, HD), (1, 0, 2, 3))
    key_groups = jnp.transpose(key_rows.reshape(TOKENS, KVH, HD), (1, 0, 2))
    value_groups = jnp.transpose(value_rows.reshape(TOKENS, KVH, HD), (1, 0, 2))

    def per_group(inputs):
        return one_group(inputs[0], inputs[1], inputs[2], inputs[3], tile_ids, tile_mask)

    outputs, query_parts, key_parts, value_parts = lax.map(per_group, (query_groups, key_groups, value_groups, grad_groups))
    attended = jnp.transpose(outputs, (1, 0, 2, 3)).reshape(TOKENS, KVH * NH * HD)
    query_grad = jnp.transpose(query_parts, (1, 0, 2, 3)).reshape(TOKENS, KVH * NH * HD)
    key_grad = jnp.transpose(key_parts, (1, 0, 2)).reshape(TOKENS, KVH * HD)
    value_grad = jnp.transpose(value_parts, (1, 0, 2)).reshape(TOKENS, KVH * HD)
    return attended, query_grad, key_grad, value_grad
```

```python
import jax
import jax.numpy as jnp
from jax import lax
from jax.experimental import pallas as pl
from jax.experimental.pallas import tpu as pltpu
from jax.sharding import PartitionSpec as P

HD = 128
TILE = 128
LOG2E = 1.4426950408889634
FAR_BELOW = -1e30
MESH = pl.DeviceIdType.MESH
VMEM = pl.BlockSpec(memory_space=pltpu.VMEM)
SMEM = pl.BlockSpec(memory_space=pltpu.SMEM)
ANY = pl.BlockSpec(memory_space=pl.ANY)


def places(ring):
    me = lax.axis_index("seq")
    z = me // 2
    core = me % 2
    right = ((z + 1) % ring) * 2 + core
    left = ((z + ring - 1) % ring) * 2 + core
    partner = z * 2 + 1 - core
    return me, z, core, right, left, partner


def meet(right, left, partner):
    barrier = pltpu.get_barrier_semaphore()
    for peer in (right, left, partner):
        pl.semaphore_signal(barrier, inc=1, device_id={"seq": peer}, device_id_type=MESH)
    pl.semaphore_wait(barrier, 3)


def chain_length(direction, chunk, ring):
    long_way = (chunk < 2) == (direction == 0)
    return ring // 2 if long_way else ring - 1 - ring // 2


def gather_kernel(ring, key_ref, value_ref, keys_out, values_out, send_sem, recv_sem, pair_send, pair_recv, own_sem):
    me, z, core, right, left, partner = places(ring)
    meet(right, left, partner)
    peers = (right, left)
    outs = (keys_out, keys_out, values_out, values_out)
    mine = (key_ref, key_ref, value_ref, value_ref)

    def part(chunk, owner):
        return outs[chunk].at[pl.ds(pl.multiple_of(owner * 2 * TILE + (chunk % 2) * TILE, TILE), TILE)]

    def own(chunk):
        return mine[chunk].at[pl.ds((chunk % 2) * TILE, TILE)]

    def owner_at(direction, hop, column):
        step = ring - hop if direction == 0 else hop
        return ((z + step) % ring) * 2 + column

    def hop_copy(direction, hop, chunk):
        owner = owner_at(direction, hop, core)
        source = own(chunk) if hop == 0 else part(chunk, owner)
        return pltpu.make_async_remote_copy(
            src_ref=source, dst_ref=part(chunk, owner),
            send_sem=send_sem.at[direction, hop, chunk], recv_sem=recv_sem.at[direction, hop, chunk],
            device_id={"seq": peers[direction]}, device_id_type=MESH)

    def arrival(direction, hop, chunk):
        owner = owner_at(direction, hop + 1, core)
        return pltpu.make_async_remote_copy(
            src_ref=part(chunk, owner), dst_ref=part(chunk, owner),
            send_sem=send_sem.at[direction, hop, chunk], recv_sem=recv_sem.at[direction, hop, chunk],
            device_id={"seq": peers[direction]}, device_id_type=MESH)

    def pair_copy(slot, chunk, source, owner):
        return pltpu.make_async_remote_copy(
            src_ref=source, dst_ref=part(chunk, owner),
            send_sem=pair_send.at[slot, chunk], recv_sem=pair_recv.at[slot, chunk],
            device_id={"seq": partner}, device_id_type=MESH)

    sent = []
    for chunk in range(4):
        for direction in range(2):
            copy = hop_copy(direction, 0, chunk)
            copy.start()
            sent.append(copy)
    pairs = []
    for chunk in range(4):
        copy = pair_copy(0, chunk, own(chunk), me)
        copy.start()
        pairs.append(copy)
    locals_ = []
    for chunk in range(4):
        copy = pltpu.make_async_copy(own(chunk), part(chunk, me), own_sem.at[chunk])
        copy.start()
        locals_.append(copy)
    for hop in range(ring // 2):
        for chunk in range(4):
            for direction in range(2):
                if hop >= chain_length(direction, chunk, ring):
                    continue
                arrival(direction, hop, chunk).wait_recv()
                if hop + 1 < chain_length(direction, chunk, ring):
                    copy = hop_copy(direction, hop + 1, chunk)
                    copy.start()
                    sent.append(copy)
                owner = owner_at(direction, hop + 1, core)
                slot = hop + 1 if direction == 0 else ring - 1 - hop
                copy = pair_copy(slot, chunk, part(chunk, owner), owner)
                copy.start()
                pairs.append(copy)
    for copy in locals_:
        copy.wait()
    for copy in sent:
        copy.wait_send()
    for slot in range(ring):
        for chunk in range(4):
            owner = owner_at(0, slot, 1 - core)
            pair_copy(slot, chunk, part(chunk, owner), owner).wait_recv()
    for copy in pairs:
        copy.wait_send()


def gather(ring, keys, values):
    rows = keys.shape[0] * ring * 2
    return pl.pallas_call(
        lambda *refs: gather_kernel(ring, *refs),
        out_shape=(jax.ShapeDtypeStruct((rows, HD), jnp.bfloat16),) * 2,
        in_specs=[VMEM, VMEM],
        out_specs=(VMEM, VMEM),
        scratch_shapes=[
            pltpu.SemaphoreType.DMA((2, ring // 2, 4)),
            pltpu.SemaphoreType.DMA((2, ring // 2, 4)),
            pltpu.SemaphoreType.DMA((ring, 4)),
            pltpu.SemaphoreType.DMA((ring, 4)),
            pltpu.SemaphoreType.DMA((4,)),
        ],
        name="gather",
        compiler_params=pltpu.CompilerParams(collective_id=0, has_side_effects=True),
    )(keys, values)


def dot(a, b, a_dim, b_dim):
    return lax.dot_general(a, b, (((a_dim,), (b_dim,)), ((), ())), preferred_element_type=jnp.float32)


def attention_kernel(heads, tiles, ids, mask, q_ref, g_ref, k_ref, v_ref,
                     att_ref, dq_ref, dk_ref, dv_ref,
                     listed, q_rows, g_rows, q_turned, g_turned, total, terms, maxima, dk_acc, dv_acc):
    factor = HD ** -0.5
    wide = heads * TILE
    me = lax.axis_index("seq")
    own_tiles = q_ref.shape[0] // TILE

    dk_acc[...] = jnp.zeros_like(dk_acc)
    dv_acc[...] = jnp.zeros_like(dv_acc)

    for a in range(own_tiles):
        rows = pl.ds(a * TILE, TILE)
        place = me * own_tiles + a
        query_tile = ids[place]
        listed[0] = place

        def build(j, n):
            ok = jnp.logical_and(mask[query_tile, ids[j]] == 1, j != place)
            listed[n] = j
            return n + ok.astype(jnp.int32)

        count = lax.fori_loop(0, tiles, build, jnp.int32(1))
        listed[count] = place
        steps = (count + 1) // 2

        for h in range(heads):
            column = pl.ds(h * HD, HD)
            block = pl.ds(h * TILE, TILE)
            q_block = q_ref[rows, column]
            g_block = g_ref[rows, column]
            q_rows[block, :] = q_block
            g_rows[block, :] = g_block
            q_turned[:, block] = q_block.T
            g_turned[:, block] = g_block.T

        def pair_of(ref, s):
            first = pl.ds(pl.multiple_of(listed[2 * s] * TILE, TILE), TILE)
            second = pl.ds(pl.multiple_of(listed[2 * s + 1] * TILE, TILE), TILE)
            return jnp.concatenate([ref[first, :], ref[second, :]], axis=0)

        def scores_of(s):
            scores = dot(pair_of(k_ref, s), q_turned[...], 1, 0) * (factor * LOG2E)
            bias = jnp.where(2 * s + 1 < count, 0.0, FAR_BELOW)
            return scores[:TILE], scores[TILE:] + bias

        def keep(s, upper, lower, top):
            upper = jnp.exp2(upper - top)
            lower = jnp.exp2(lower - top)
            both = jnp.concatenate([upper, lower], axis=0)
            terms[s] = both
            maxima[s] = top
            return jnp.sum(both, axis=0, keepdims=True), dot(pair_of(v_ref, s), both.astype(jnp.bfloat16), 0, 0)

        upper, lower = scores_of(0)
        key_place = lax.broadcasted_iota(jnp.int32, (TILE, wide), 0)
        query_place = lax.broadcasted_iota(jnp.int32, (TILE, wide), 1) % TILE
        upper = jnp.where(query_place >= key_place, upper, FAR_BELOW)
        top = jnp.max(jnp.maximum(upper, lower), axis=0, keepdims=True)
        share, weighted = keep(0, upper, lower, top)
        total[...] = weighted

        def forward(s, carried):
            top, share = carried
            upper, lower = scores_of(s)
            new_top = jnp.maximum(top, jnp.max(jnp.maximum(upper, lower), axis=0, keepdims=True))
            shrink = jnp.exp2(top - new_top)
            more, weighted = keep(s, upper, lower, new_top)
            total[...] = total[...] * shrink + weighted
            return new_top, share * shrink + more

        top, share = lax.fori_loop(1, steps, forward, (top, share))
        attended = (total[...] / share).astype(jnp.bfloat16)
        delta = jnp.sum(g_turned[...].astype(jnp.float32) * attended.astype(jnp.float32), axis=0, keepdims=True)
        log_total = top + jnp.log2(share)
        for h in range(heads):
            att_ref[rows, pl.ds(h * HD, HD)] = attended[:, h * TILE:(h + 1) * TILE].T

        total[...] = jnp.zeros_like(total)

        def backward(s, carried):
            probs = terms[s] * jnp.exp2(maxima[s] - log_total)
            dprobs = dot(pair_of(v_ref, s), g_turned[...], 1, 0)
            dscores = (probs * (dprobs - delta)).astype(jnp.bfloat16)
            dv_part = dot(probs.astype(jnp.bfloat16), g_rows[...], 1, 0)
            dk_part = dot(dscores, q_rows[...], 1, 0)
            first = pl.ds(pl.multiple_of(listed[2 * s] * TILE, TILE), TILE)
            second = pl.ds(pl.multiple_of(listed[2 * s + 1] * TILE, TILE), TILE)
            dv_acc[first, :] += dv_part[:TILE]
            dv_acc[second, :] += dv_part[TILE:]
            dk_acc[first, :] += dk_part[:TILE]
            dk_acc[second, :] += dk_part[TILE:]
            total[...] += dot(pair_of(k_ref, s), dscores, 0, 0)
            return carried

        lax.fori_loop(0, steps, backward, jnp.int32(0))
        for h in range(heads):
            dq_ref[rows, pl.ds(h * HD, HD)] = (total[:, h * TILE:(h + 1) * TILE] * factor).T

    dk_ref[...] = (dk_acc[...] * factor).astype(jnp.bfloat16)
    dv_ref[...] = dv_acc[...].astype(jnp.bfloat16)


def attention(queries, grads, keys, values, ids, mask):
    rows, width = queries.shape
    heads = width // HD
    key_total = keys.shape[0]
    tiles = key_total // TILE
    wide = heads * TILE
    return pl.pallas_call(
        lambda *refs: attention_kernel(heads, tiles, *refs),
        out_shape=(
            jax.ShapeDtypeStruct((rows, width), jnp.bfloat16),
            jax.ShapeDtypeStruct((rows, width), jnp.float32),
            jax.ShapeDtypeStruct((key_total, HD), jnp.bfloat16),
            jax.ShapeDtypeStruct((key_total, HD), jnp.bfloat16),
        ),
        in_specs=[SMEM, SMEM, VMEM, VMEM, VMEM, VMEM],
        out_specs=(VMEM,) * 4,
        scratch_shapes=[
            pltpu.SMEM((tiles + 8,), jnp.int32),
            pltpu.VMEM((wide, HD), jnp.bfloat16),
            pltpu.VMEM((wide, HD), jnp.bfloat16),
            pltpu.VMEM((HD, wide), jnp.bfloat16),
            pltpu.VMEM((HD, wide), jnp.bfloat16),
            pltpu.VMEM((HD, wide), jnp.float32),
            pltpu.VMEM((tiles // 2, 2 * TILE, wide), jnp.float32),
            pltpu.VMEM((tiles // 2, 1, wide), jnp.float32),
            pltpu.VMEM((key_total, HD), jnp.float32),
            pltpu.VMEM((key_total, HD), jnp.float32),
        ],
        name="attention",
    )(ids, mask, queries, grads, keys, values)


def scatter_kernel(ring, dk_ref, dv_ref, dk_out, dv_out, landed, outgoing, pair_in,
                   send_sem, recv_sem, pair_send, pair_recv):
    me, z, core, right, left, partner = places(ring)
    meet(right, left, partner)
    peers = (right, left)
    sources = (dk_ref, dk_ref, dv_ref, dv_ref)

    def rows_of(chunk, owner):
        return pl.ds(pl.multiple_of(owner * 2 * TILE + (chunk % 2) * TILE, TILE), TILE)

    def pair_copy(slot, chunk):
        chip = (z + slot) % ring
        return pltpu.make_async_remote_copy(
            src_ref=sources[chunk].at[rows_of(chunk, chip * 2 + 1 - core)], dst_ref=pair_in.at[slot, chunk],
            send_sem=pair_send.at[slot, chunk], recv_sem=pair_recv.at[slot, chunk],
            device_id={"seq": partner}, device_id_type=MESH)

    def ring_copy(direction, hop, chunk):
        return pltpu.make_async_remote_copy(
            src_ref=outgoing.at[direction, hop, chunk], dst_ref=landed.at[direction, hop, chunk],
            send_sem=send_sem.at[direction, hop, chunk], recv_sem=recv_sem.at[direction, hop, chunk],
            device_id={"seq": peers[direction]}, device_id_type=MESH)

    order = []
    for hop in range(ring // 2):
        for chunk in range(4):
            for direction in range(2):
                length = chain_length(direction, chunk, ring)
                if hop < length:
                    away = length - hop
                    order.append((away if direction == 0 else ring - away, chunk))
    order += [(0, chunk) for chunk in range(4)]
    seen = []
    for item in order:
        if item not in seen:
            seen.append(item)
    pairs = []
    for slot, chunk in seen:
        copy = pair_copy(slot, chunk)
        copy.start()
        pairs.append(copy)

    def local_sum(slot, chunk):
        pair_copy(slot, chunk).wait_recv()
        chip = (z + slot) % ring
        return (sources[chunk][rows_of(chunk, chip * 2 + core), :].astype(jnp.float32)
                + pair_in[slot, chunk].astype(jnp.float32))

    sent = []
    ends = {}
    for hop in range(ring // 2):
        for chunk in range(4):
            for direction in range(2):
                length = chain_length(direction, chunk, ring)
                if hop >= length:
                    continue
                away = length - hop
                value = local_sum(away if direction == 0 else ring - away, chunk)
                if hop > 0:
                    ring_copy(direction, hop - 1, chunk).wait_recv()
                    value = value + landed[direction, hop - 1, chunk].astype(jnp.float32)
                outgoing[direction, hop, chunk] = value.astype(jnp.bfloat16)
                copy = ring_copy(direction, hop, chunk)
                copy.start()
                sent.append(copy)
    for chunk in range(4):
        value = local_sum(0, chunk)
        for direction in (0, 1):
            last = chain_length(direction, chunk, ring) - 1
            ring_copy(direction, last, chunk).wait_recv()
            value = value + landed[direction, last, chunk].astype(jnp.float32)
        out = dk_out if chunk < 2 else dv_out
        out[pl.ds((chunk % 2) * TILE, TILE), :] = value
    for copy in sent:
        copy.wait_send()
    for copy in pairs:
        copy.wait_send()


def scatter(ring, dk, dv):
    rows = dk.shape[0] // (2 * ring)
    hops = ring // 2
    return pl.pallas_call(
        lambda *refs: scatter_kernel(ring, *refs),
        out_shape=(jax.ShapeDtypeStruct((rows, HD), jnp.float32),) * 2,
        in_specs=[VMEM, VMEM],
        out_specs=(VMEM, VMEM),
        scratch_shapes=[
            pltpu.VMEM((2, hops, 4, TILE, HD), jnp.bfloat16),
            pltpu.VMEM((2, hops, 4, TILE, HD), jnp.bfloat16),
            pltpu.VMEM((ring, 4, TILE, HD), jnp.bfloat16),
            pltpu.SemaphoreType.DMA((2, hops, 4)),
            pltpu.SemaphoreType.DMA((2, hops, 4)),
            pltpu.SemaphoreType.DMA((ring, 4)),
            pltpu.SemaphoreType.DMA((ring, 4)),
        ],
        name="scatter",
        compiler_params=pltpu.CompilerParams(collective_id=1, has_side_effects=True),
    )(dk, dv)


def solution(mesh):
    ring = mesh.shape["seq"] // 2

    def per_device(queries, key_rows, value_rows, out_grad, tile_ids, tile_mask):
        keys, values = gather(ring, key_rows, value_rows)
        attended, query_grad, dk, dv = attention(queries, out_grad, keys, values, tile_ids, tile_mask)
        key_grad, value_grad = scatter(ring, dk, dv)
        return attended, query_grad, key_grad, value_grad

    spec = P(("batch", "seq"), "head")
    return jax.shard_map(
        per_device,
        mesh=mesh,
        in_specs=(spec, spec, spec, spec, P("batch"), P("batch", None)),
        out_specs=(spec,) * 4,
        check_vma=False,
    )
```

```python
import jax
import jax.numpy as jnp
from jax import lax
from jax.experimental import pallas as pl
from jax.experimental.pallas import tpu as pltpu
from jax.sharding import PartitionSpec as P

HD = 128
TILE = 128
BLOCK = 2 * TILE
LOG2E = 1.4426950408889634
FAR_BELOW = -1e30
MESH = pl.DeviceIdType.MESH
VMEM = pl.BlockSpec(memory_space=pltpu.VMEM)
SMEM = pl.BlockSpec(memory_space=pltpu.SMEM)
RING = 8


def dot(a, b):
    return lax.dot_general(a, b, (((1,), (0,)), ((), ())), preferred_element_type=jnp.float32)


def kernel(heads, ids, mask, q_ref, g_ref, k_ref, v_ref, att_ref, dq_ref, dk_ref, dv_ref,
           kv, q_rows, g_rows, q_turned, g_turned, bias, terms, maxima, total, top_ref, share_ref, delta_ref,
           own_part, pair_out, pair_in, outgoing, landed,
           gather_send, gather_recv, share_send, share_recv, pair_send, pair_recv, ring_send, ring_recv):
    factor = HD ** -0.5
    wide = 2 * heads * TILE
    columns = [slice(n * BLOCK, (n + 1) * BLOCK) for n in range(wide // BLOCK)]
    blocks_per_tile = len(columns) // 2
    me = lax.axis_index("seq")
    z = me // 2
    core = me % 2
    peers = (((z + 1) % RING) * 2 + core, ((z + RING - 1) % RING) * 2 + core)
    partner = z * 2 + 1 - core

    barrier = pltpu.get_barrier_semaphore()
    for peer in peers + (partner,):
        pl.semaphore_signal(barrier, inc=1, device_id={"seq": peer}, device_id_type=MESH)
    pl.semaphore_wait(barrier, 3)

    def own_chunk(chunk):
        return (k_ref if chunk < 2 else v_ref).at[pl.ds((chunk % 2) * TILE, TILE)]

    def hop_copy(direction, hop, chunk, source=None):
        offset = RING - hop if direction == 0 else hop
        place = kv.at[((z + offset) % RING) * 2 + core, chunk]
        return pltpu.make_async_remote_copy(
            src_ref=place if source is None else source, dst_ref=place,
            send_sem=gather_send.at[direction, hop, chunk], recv_sem=gather_recv.at[direction, hop, chunk],
            device_id={"seq": peers[direction]}, device_id_type=MESH)

    def share_copy(back, chunk, column, source=None):
        place = kv.at[((z + RING - back) % RING) * 2 + column, chunk]
        return pltpu.make_async_remote_copy(
            src_ref=place if source is None else source, dst_ref=place,
            send_sem=share_send.at[back, chunk], recv_sem=share_recv.at[back, chunk],
            device_id={"seq": partner}, device_id_type=MESH)

    for n in range(4):
        for direction in range(2):
            chunk = (n + 2 * direction) % 4
            hop_copy(direction, 0, chunk, own_chunk(chunk)).start()
    for chunk in range(4):
        share_copy(0, chunk, core, own_chunk(chunk)).start()
    for r in range(2):
        kv[me, r] = k_ref[pl.ds(r * TILE, TILE), :]
        kv[me, 2 + r] = v_ref[pl.ds(r * TILE, TILE), :]

    def gather_slot(j):
        hop = j // 4
        for direction in range(2):
            chunk = (j + 2 * direction) % 4
            offset = RING - hop - 1 if direction == 0 else hop + 1
            place = kv.at[((z + offset) % RING) * 2 + core, chunk]
            pltpu.make_async_remote_copy(
                src_ref=place, dst_ref=place,
                send_sem=gather_send.at[direction, hop, chunk], recv_sem=gather_recv.at[direction, hop, chunk],
                device_id={"seq": peers[direction]}, device_id_type=MESH).wait_recv()

            @pl.when(j < 10)
            def _():
                hop_copy(direction, hop + 1, chunk).start()

            share_copy((RING - offset) % RING, chunk, core).start()

    row = lax.broadcasted_iota(jnp.int32, (TILE, TILE), 0)
    lane = lax.broadcasted_iota(jnp.int32, (TILE, TILE), 1)
    bias[0] = jnp.zeros((TILE, TILE), jnp.float32)
    bias[1] = jnp.where(lane >= row, 0.0, FAR_BELOW)
    bias[2] = jnp.full((TILE, TILE), FAR_BELOW, jnp.float32)
    for a in range(2):
        for h in range(heads):
            block = pl.ds((a * heads + h) * TILE, TILE)
            q_block = q_ref[pl.ds(a * TILE, TILE), pl.ds(h * HD, HD)]
            g_block = g_ref[pl.ds(a * TILE, TILE), pl.ds(h * HD, HD)]
            q_rows[block, :] = q_block
            g_rows[block, :] = g_block
            q_turned[:, block] = q_block.T
            g_turned[:, block] = g_block.T
    top_ref[...] = jnp.full_like(top_ref, FAR_BELOW)
    share_ref[...] = jnp.zeros_like(share_ref)
    total[...] = jnp.zeros_like(total)

    def bias_block(owner, r, a):
        state = jnp.where(mask[ids[me * 2 + a], ids[owner * 2 + r]] == 1, 0, 2)
        state = jnp.where(owner * 2 + r == me * 2 + a, 1, state)
        one = bias[state]
        return jnp.concatenate([one] * (BLOCK // TILE), axis=1)

    def forward_unit(owner):
        keys = kv[owner, 0:2].reshape(BLOCK, HD)
        values_turned = kv[owner, 2:4].reshape(BLOCK, HD).T
        biases = [jnp.concatenate([bias_block(owner, 0, a), bias_block(owner, 1, a)], axis=0) for a in range(2)]
        for n, column in enumerate(columns):
            scores = dot(keys, q_turned[:, column]) * (factor * LOG2E) + biases[n // blocks_per_tile]
            old = top_ref[:, column]
            top = jnp.maximum(old, jnp.max(scores, axis=0, keepdims=True))
            shrink = jnp.exp2(old - top)
            probs = jnp.exp2(scores - top)
            terms[owner, :, column] = probs
            maxima[owner, :, column] = top
            top_ref[:, column] = top
            share_ref[:, column] = share_ref[:, column] * shrink + jnp.sum(probs, axis=0, keepdims=True)
            total[:, column] = total[:, column] * shrink + dot(values_turned, probs.astype(jnp.bfloat16))

    def forward_step(j, carried):
        unit = jnp.where(j < 2, j, j - 2)

        @pl.when(jnp.logical_or(j < 2, j >= 4))
        def _():
            rest = jnp.maximum(unit - 2, 0)
            near = rest // 4
            which = rest % 4
            back = jnp.where(which % 2 == 0, near + 1, RING - 1 - near)
            other = jnp.where(near == 3, which, which // 2)
            back = jnp.where(unit < 2, 0, back)
            other = jnp.where(unit < 2, unit, other)
            column = jnp.where(other == 1, 1 - core, core)

            @pl.when(other == 1)
            def _():
                for chunk in range(4):
                    share_copy(back, chunk, 1 - core).wait_recv()

            forward_unit(((z + RING - back) % RING) * 2 + column)

        @pl.when(j < 14)
        def _():
            gather_slot(j)

        return carried

    lax.fori_loop(0, 18, forward_step, 0)

    attended = (total[...] / share_ref[...]).astype(jnp.bfloat16)
    delta_ref[...] = jnp.sum(g_turned[...].astype(jnp.float32) * attended.astype(jnp.float32), axis=0, keepdims=True)
    top_ref[...] = top_ref[...] + jnp.log2(share_ref[...])
    for a in range(2):
        for h in range(heads):
            n = a * heads + h
            att_ref[pl.ds(a * TILE, TILE), pl.ds(h * HD, HD)] = attended[:, n * TILE:(n + 1) * TILE].T
    total[...] = jnp.zeros_like(total)

    def pair_copy(n):
        return pltpu.make_async_remote_copy(
            src_ref=pair_out.at[n], dst_ref=pair_in.at[n], send_sem=pair_send.at[n], recv_sem=pair_recv.at[n],
            device_id={"seq": partner}, device_id_type=MESH)

    def ring_copy(direction, hop, which):
        return pltpu.make_async_remote_copy(
            src_ref=outgoing.at[direction, hop, which], dst_ref=landed.at[direction, hop, which],
            send_sem=ring_send.at[direction, hop, which], recv_sem=ring_recv.at[direction, hop, which],
            device_id={"seq": peers[direction]}, device_id_type=MESH)

    def pass_on(direction, hop, which, n):
        value = own_part[n, which] + pair_in[n, which].astype(jnp.float32)
        outgoing[direction, hop, which] = value.astype(jnp.bfloat16)

        @pl.when(hop > 0)
        def _():
            before = jnp.maximum(hop - 1, 0)
            ring_copy(direction, before, which).wait_recv()
            outgoing[direction, hop, which] = (value + landed[direction, before, which].astype(jnp.float32)).astype(jnp.bfloat16)

        ring_copy(direction, hop, which).start()

    def backward_unit(owner):
        keys_turned = kv[owner, 0:2].reshape(BLOCK, HD).T
        values = kv[owner, 2:4].reshape(BLOCK, HD)
        probs_all, dscores_all = [], []
        for n, column in enumerate(columns):
            probs = terms[owner, :, column] * jnp.exp2(maxima[owner, :, column] - top_ref[:, column])
            dprobs = dot(values, g_turned[:, column])
            dscores = (probs * (dprobs - delta_ref[:, column])).astype(jnp.bfloat16)
            probs_all.append(probs.astype(jnp.bfloat16))
            dscores_all.append(dscores)
            total[:, column] += dot(keys_turned, dscores)
        dk = dot(jnp.concatenate(dscores_all, axis=1), q_rows[...]) * factor
        dv = dot(jnp.concatenate(probs_all, axis=1), g_rows[...])
        return dk, dv

    def backward_step(i, carried):
        n = i // 2
        back = jnp.where(n % 2 == 1, RING - (7 - n) // 2, (8 - n) // 2) % RING
        column = jnp.where(i % 2 == 0, 1 - core, core)
        dk, dv = backward_unit(((z + RING - back) % RING) * 2 + column)

        @pl.when(i % 2 == 0)
        def _():
            pair_out[n, 0] = dk.astype(jnp.bfloat16)
            pair_out[n, 1] = dv.astype(jnp.bfloat16)
            pair_copy(n).start()

        @pl.when(i % 2 == 1)
        def _():
            own_part[n, 0] = dk
            own_part[n, 1] = dv

        @pl.when(i % 4 == 2)
        def _():
            burst = i // 4

            @pl.when(burst == 0)
            def _():
                pair_copy(0).wait_recv()

            @pl.when(burst > 0)
            def _():
                pair_copy(2 * burst - 1).wait_recv()
                pair_copy(2 * burst).wait_recv()

            right = jnp.maximum(2 * burst - 1, 0)
            pass_on(0, burst, 0, right)
            pass_on(1, burst, 1, 2 * burst)

            @pl.when(burst > 0)
            def _():
                pass_on(0, jnp.maximum(burst - 1, 0), 1, right)
                pass_on(1, jnp.maximum(burst - 1, 0), 0, 2 * burst)

        return carried

    lax.fori_loop(0, 16, backward_step, 0)

    for a in range(2):
        for h in range(heads):
            n = a * heads + h
            dq_ref[pl.ds(a * TILE, TILE), pl.ds(h * HD, HD)] = (total[:, n * TILE:(n + 1) * TILE] * factor).T

    pair_copy(7).wait_recv()
    for which, out in ((1, dv_ref), (0, dk_ref)):
        value = own_part[7, which] + pair_in[7, which].astype(jnp.float32)
        for direction in range(2):
            last = 3 if which == direction else 2
            ring_copy(direction, last, which).wait_recv()
            value = value + landed[direction, last, which].astype(jnp.float32)
        out[...] = value

    for direction in range(2):
        for hop in range(4):
            for chunk in range(4):
                if hop < 3 or (chunk < 2) == (direction == 0):
                    hop_copy(direction, hop, chunk).wait_send()
            for which in range(2):
                if hop < 3 or which == direction:
                    ring_copy(direction, hop, which).wait_send()
    for back in range(RING):
        pair_copy(back).wait_send()
        for chunk in range(4):
            share_copy(back, chunk, core).wait_send()


def fused(queries, grads, keys, values, ids, mask):
    rows, width = queries.shape
    heads = width // HD
    devices = 2 * RING
    wide = 2 * heads * TILE
    f32, bf16 = jnp.float32, jnp.bfloat16
    dma = pltpu.SemaphoreType.DMA
    return pl.pallas_call(
        lambda *refs: kernel(heads, *refs),
        out_shape=(
            jax.ShapeDtypeStruct((rows, width), bf16),
            jax.ShapeDtypeStruct((rows, width), f32),
            jax.ShapeDtypeStruct((rows, HD), f32),
            jax.ShapeDtypeStruct((rows, HD), f32),
        ),
        in_specs=[SMEM, SMEM, VMEM, VMEM, VMEM, VMEM],
        out_specs=(VMEM,) * 4,
        scratch_shapes=[
            pltpu.VMEM((devices, 4, TILE, HD), bf16),
            pltpu.VMEM((wide, HD), bf16),
            pltpu.VMEM((wide, HD), bf16),
            pltpu.VMEM((HD, wide), bf16),
            pltpu.VMEM((HD, wide), bf16),
            pltpu.VMEM((3, TILE, TILE), f32),
            pltpu.VMEM((devices, BLOCK, wide), f32),
            pltpu.VMEM((devices, 1, wide), f32),
            pltpu.VMEM((HD, wide), f32),
            pltpu.VMEM((1, wide), f32),
            pltpu.VMEM((1, wide), f32),
            pltpu.VMEM((1, wide), f32),
            pltpu.VMEM((RING, 2, BLOCK, HD), f32),
            pltpu.VMEM((RING, 2, BLOCK, HD), bf16),
            pltpu.VMEM((RING, 2, BLOCK, HD), bf16),
            pltpu.VMEM((2, 4, 2, BLOCK, HD), bf16),
            pltpu.VMEM((2, 4, 2, BLOCK, HD), bf16),
            dma((2, 4, 4)),
            dma((2, 4, 4)),
            dma((RING, 4)),
            dma((RING, 4)),
            dma((RING,)),
            dma((RING,)),
            dma((2, 4, 2)),
            dma((2, 4, 2)),
        ],
        name="fused",
        compiler_params=pltpu.CompilerParams(collective_id=0, has_side_effects=True),
    )(ids, mask, queries, grads, keys, values)


def solution(mesh):
    def per_device(queries, key_rows, value_rows, out_grad, tile_ids, tile_mask):
        return fused(queries, out_grad, key_rows, value_rows, tile_ids, tile_mask)

    spec = P(("batch", "seq"), "head")
    return jax.shard_map(
        per_device,
        mesh=mesh,
        in_specs=(spec, spec, spec, spec, P("batch"), P("batch", None)),
        out_specs=(spec,) * 4,
        check_vma=False,
    )
```

```python
import jax
import jax.numpy as jnp
from jax import lax
from jax.experimental import pallas as pl
from jax.experimental.pallas import tpu as pltpu
from jax.sharding import PartitionSpec as P

HD = 128
TILE = 128
BLOCK = 2 * TILE
ONES = 16
LOG2E = 1.4426950408889634
FAR_BELOW = -1e30
MESH = pl.DeviceIdType.MESH
VMEM = pl.BlockSpec(memory_space=pltpu.VMEM)
SMEM = pl.BlockSpec(memory_space=pltpu.SMEM)
RING = 8


def dot(a, b):
    return lax.dot_general(a, b, (((1,), (0,)), ((), ())), preferred_element_type=jnp.float32)


def kernel(heads, ids, mask, q_ref, g_ref, k_ref, v_ref, att_ref, dq_ref, dk_ref, dv_ref,
           kv, q_rows, g_rows, q_turned, g_turned, terms, maxima, total, top_ref,
           own_part, pair_out, pair_in, outgoing, landed,
           gather_send, gather_recv, share_send, share_recv, pair_send, pair_recv, ring_send, ring_recv):
    factor = HD ** -0.5
    wide = 2 * heads * TILE
    columns = [slice(n * BLOCK, (n + 1) * BLOCK) for n in range(wide // BLOCK)]
    blocks_per_tile = len(columns) // 2
    me = lax.axis_index("seq")
    z = me // 2
    core = me % 2
    peers = (((z + 1) % RING) * 2 + core, ((z + RING - 1) % RING) * 2 + core)
    partner = z * 2 + 1 - core

    barrier = pltpu.get_barrier_semaphore()
    for peer in peers + (partner,):
        pl.semaphore_signal(barrier, inc=1, device_id={"seq": peer}, device_id_type=MESH)
    pl.semaphore_wait(barrier, 3)

    def own_chunk(chunk):
        return (k_ref if chunk < 2 else v_ref).at[pl.ds((chunk % 2) * TILE, TILE)]

    def hop_copy(direction, hop, chunk, source=None):
        offset = RING - hop if direction == 0 else hop
        place = kv.at[((z + offset) % RING) * 2 + core, chunk]
        return pltpu.make_async_remote_copy(
            src_ref=place if source is None else source, dst_ref=place,
            send_sem=gather_send.at[direction, hop, chunk], recv_sem=gather_recv.at[direction, hop, chunk],
            device_id={"seq": peers[direction]}, device_id_type=MESH)

    def share_copy(back, chunk, column, source=None):
        place = kv.at[((z + RING - back) % RING) * 2 + column, chunk]
        return pltpu.make_async_remote_copy(
            src_ref=place if source is None else source, dst_ref=place,
            send_sem=share_send.at[back, chunk], recv_sem=share_recv.at[back, chunk],
            device_id={"seq": partner}, device_id_type=MESH)

    for n in range(4):
        for direction in range(2):
            chunk = (n + 2 * direction) % 4
            hop_copy(direction, 0, chunk, own_chunk(chunk)).start()
    for chunk in range(4):
        share_copy(0, chunk, core, own_chunk(chunk)).start()
    for r in range(2):
        kv[me, r] = k_ref[pl.ds(r * TILE, TILE), :]
        kv[me, 2 + r] = v_ref[pl.ds(r * TILE, TILE), :]

    def gather_slot(j):
        hop = j // 4
        for direction in range(2):
            chunk = (j + 2 * direction) % 4
            offset = RING - hop - 1 if direction == 0 else hop + 1
            place = kv.at[((z + offset) % RING) * 2 + core, chunk]
            pltpu.make_async_remote_copy(
                src_ref=place, dst_ref=place,
                send_sem=gather_send.at[direction, hop, chunk], recv_sem=gather_recv.at[direction, hop, chunk],
                device_id={"seq": peers[direction]}, device_id_type=MESH).wait_recv()

            @pl.when(j < 10)
            def _():
                hop_copy(direction, hop + 1, chunk).start()

            share_copy((RING - offset) % RING, chunk, core).start()

    for a in range(2):
        for h in range(heads):
            block = pl.ds((a * heads + h) * TILE, TILE)
            q_block = q_ref[pl.ds(a * TILE, TILE), pl.ds(h * HD, HD)]
            g_block = g_ref[pl.ds(a * TILE, TILE), pl.ds(h * HD, HD)]
            q_rows[block, :] = q_block
            g_rows[block, :] = g_block
            scaled = q_block.T.astype(jnp.float32) * (factor * LOG2E)
            coarse = scaled.astype(jnp.bfloat16)
            q_turned[:HD, block] = coarse
            q_turned[HD:, block] = (scaled - coarse.astype(jnp.float32)).astype(jnp.bfloat16)
            g_turned[:HD, block] = g_block.T

    def bias_of(owner, r, a):
        return jnp.where(mask[ids[me * 2 + a], ids[owner * 2 + r]] == 1, 0.0, FAR_BELOW)

    def forward_unit(owner, first):
        keys = kv[owner, 0:2].reshape(BLOCK, HD)
        keys = jnp.concatenate([keys, keys], axis=1)
        values_turned = jnp.concatenate(
            [kv[owner, 2:4].reshape(BLOCK, HD).T, jnp.ones((ONES, BLOCK), jnp.bfloat16)], axis=0)
        biases = [[bias_of(owner, r, a) for a in range(2)] for r in range(2)]

        def scores_of(column):
            return dot(keys, q_turned[:, column])

        ahead = scores_of(columns[0])
        for n, column in enumerate(columns):
            scores = ahead
            if n + 1 < len(columns):
                ahead = scores_of(columns[n + 1])
            a = n // blocks_per_tile
            halves = [scores[r * TILE:(r + 1) * TILE] for r in range(2)]
            if first:
                row = lax.broadcasted_iota(jnp.int32, (TILE, BLOCK), 0)
                lane = lax.broadcasted_iota(jnp.int32, (TILE, BLOCK), 1) % TILE
                halves[a] = jnp.where(lane >= row, halves[a], FAR_BELOW)
            tops = [jnp.max(halves[r], axis=0, keepdims=True) + biases[r][a] for r in range(2)]
            top = jnp.maximum(tops[0], tops[1])
            if not first:
                old = top_ref[:, column]
                top = jnp.maximum(old, top)
            probs = jnp.concatenate([jnp.exp2(halves[r] - (top - biases[r][a])) for r in range(2)], axis=0)
            terms[owner, :, column] = probs
            maxima[owner, :, column] = top
            top_ref[:, column] = top
            weighted = dot(values_turned, probs.astype(jnp.bfloat16))
            total[:, column] = weighted if first else total[:, column] * jnp.exp2(old - top) + weighted

    def forward_step(j, carried):
        unit = jnp.where(j < 2, 1, j - 2)

        @pl.when(jnp.logical_or(j == 1, j >= 4))
        def _():
            rest = jnp.maximum(unit - 2, 0)
            near = rest // 4
            which = rest % 4
            back = jnp.where(which % 2 == 0, near + 1, RING - 1 - near)
            other = jnp.where(near == 3, which, which // 2)
            back = jnp.where(unit < 2, 0, back)
            other = jnp.where(unit < 2, unit, other)
            column = jnp.where(other == 1, 1 - core, core)

            @pl.when(other == 1)
            def _():
                for chunk in range(4):
                    share_copy(back, chunk, 1 - core).wait_recv()

            forward_unit(((z + RING - back) % RING) * 2 + column, False)

        @pl.when(j < 14)
        def _():
            gather_slot(j)

        return carried

    forward_unit(me, True)
    lax.fori_loop(0, 18, forward_step, 0)

    attended = (total[:HD] / total[HD:HD + 1]).astype(jnp.bfloat16)
    rest = -jnp.sum(g_turned[:HD].astype(jnp.float32) * attended.astype(jnp.float32), axis=0, keepdims=True)
    top_ref[...] = top_ref[...] + jnp.log2(total[HD:HD + 1])
    place = lax.broadcasted_iota(jnp.int32, (ONES, 1), 0)
    extra = jnp.zeros((ONES, wide), jnp.float32)
    for n in range(3):
        term = rest.astype(jnp.bfloat16).astype(jnp.float32)
        extra = jnp.where(place == n, term, extra)
        rest = rest - term
    g_turned[HD:HD + ONES] = extra.astype(jnp.bfloat16)
    g_turned[HD + ONES:] = jnp.zeros((HD - ONES, wide), jnp.bfloat16)
    for a in range(2):
        for h in range(heads):
            n = a * heads + h
            att_ref[pl.ds(a * TILE, TILE), pl.ds(h * HD, HD)] = attended[:, n * TILE:(n + 1) * TILE].T
    total[:HD] = jnp.zeros((HD, wide), jnp.float32)

    def pair_copy(n):
        return pltpu.make_async_remote_copy(
            src_ref=pair_out.at[n], dst_ref=pair_in.at[n], send_sem=pair_send.at[n], recv_sem=pair_recv.at[n],
            device_id={"seq": partner}, device_id_type=MESH)

    def ring_copy(direction, hop, which):
        return pltpu.make_async_remote_copy(
            src_ref=outgoing.at[direction, hop, which], dst_ref=landed.at[direction, hop, which],
            send_sem=ring_send.at[direction, hop, which], recv_sem=ring_recv.at[direction, hop, which],
            device_id={"seq": peers[direction]}, device_id_type=MESH)

    def pass_on(direction, hop, which, n):
        value = own_part[n, which] + pair_in[n, which].astype(jnp.float32)
        outgoing[direction, hop, which] = value.astype(jnp.bfloat16)

        @pl.when(hop > 0)
        def _():
            before = jnp.maximum(hop - 1, 0)
            ring_copy(direction, before, which).wait_recv()
            outgoing[direction, hop, which] = (value + landed[direction, before, which].astype(jnp.float32)).astype(jnp.bfloat16)

        ring_copy(direction, hop, which).start()

    def backward_unit(owner):
        keys_turned = kv[owner, 0:2].reshape(BLOCK, HD).T
        values = jnp.concatenate(
            [kv[owner, 2:4].reshape(BLOCK, HD),
             (lax.broadcasted_iota(jnp.int32, (BLOCK, HD), 1) < 3).astype(jnp.bfloat16)], axis=1)
        probs_all, dscores_all = [], []

        def dprobs_of(column):
            return dot(values, g_turned[:, column])

        ahead = dprobs_of(columns[0])
        for n, column in enumerate(columns):
            dprobs = ahead
            if n + 1 < len(columns):
                ahead = dprobs_of(columns[n + 1])
            probs = terms[owner, :, column] * jnp.exp2(maxima[owner, :, column] - top_ref[:, column])
            dscores = (probs * dprobs).astype(jnp.bfloat16)
            probs_all.append(probs.astype(jnp.bfloat16))
            dscores_all.append(dscores)
            total[:HD, column] += dot(keys_turned, dscores)
        dk = dot(jnp.concatenate(dscores_all, axis=1), q_rows[...]) * factor
        dv = dot(jnp.concatenate(probs_all, axis=1), g_rows[...])
        return dk, dv

    def backward_step(i, carried):
        n = i // 2
        back = jnp.where(n % 2 == 1, RING - (7 - n) // 2, (8 - n) // 2) % RING
        column = jnp.where(i % 2 == 0, 1 - core, core)
        dk, dv = backward_unit(((z + RING - back) % RING) * 2 + column)

        @pl.when(i % 2 == 0)
        def _():
            pair_out[n, 0] = dk.astype(jnp.bfloat16)
            pair_out[n, 1] = dv.astype(jnp.bfloat16)
            pair_copy(n).start()

        @pl.when(i % 2 == 1)
        def _():
            own_part[n, 0] = dk
            own_part[n, 1] = dv

        @pl.when(i % 4 == 2)
        def _():
            burst = i // 4

            @pl.when(burst == 0)
            def _():
                pair_copy(0).wait_recv()

            @pl.when(burst > 0)
            def _():
                pair_copy(2 * burst - 1).wait_recv()
                pair_copy(2 * burst).wait_recv()

            right = jnp.maximum(2 * burst - 1, 0)
            pass_on(0, burst, 0, right)
            pass_on(1, burst, 1, 2 * burst)

            @pl.when(burst > 0)
            def _():
                pass_on(0, jnp.maximum(burst - 1, 0), 1, right)
                pass_on(1, jnp.maximum(burst - 1, 0), 0, 2 * burst)

        return carried

    lax.fori_loop(0, 16, backward_step, 0)

    for a in range(2):
        for h in range(heads):
            n = a * heads + h
            dq_ref[pl.ds(a * TILE, TILE), pl.ds(h * HD, HD)] = (total[:HD, n * TILE:(n + 1) * TILE] * factor).T

    pair_copy(7).wait_recv()
    for which, out in ((1, dv_ref), (0, dk_ref)):
        value = own_part[7, which] + pair_in[7, which].astype(jnp.float32)
        for direction in range(2):
            last = 3 if which == direction else 2
            ring_copy(direction, last, which).wait_recv()
            value = value + landed[direction, last, which].astype(jnp.float32)
        out[...] = value

    for direction in range(2):
        for hop in range(4):
            for chunk in range(4):
                if hop < 3 or (chunk < 2) == (direction == 0):
                    hop_copy(direction, hop, chunk).wait_send()
            for which in range(2):
                if hop < 3 or which == direction:
                    ring_copy(direction, hop, which).wait_send()
    for back in range(RING):
        pair_copy(back).wait_send()
        for chunk in range(4):
            share_copy(back, chunk, core).wait_send()


def fused(queries, grads, keys, values, ids, mask):
    rows, width = queries.shape
    heads = width // HD
    devices = 2 * RING
    wide = 2 * heads * TILE
    f32, bf16 = jnp.float32, jnp.bfloat16
    dma = pltpu.SemaphoreType.DMA
    return pl.pallas_call(
        lambda *refs: kernel(heads, *refs),
        out_shape=(
            jax.ShapeDtypeStruct((rows, width), bf16),
            jax.ShapeDtypeStruct((rows, width), f32),
            jax.ShapeDtypeStruct((rows, HD), f32),
            jax.ShapeDtypeStruct((rows, HD), f32),
        ),
        in_specs=[SMEM, SMEM, VMEM, VMEM, VMEM, VMEM],
        out_specs=(VMEM,) * 4,
        scratch_shapes=[
            pltpu.VMEM((devices, 4, TILE, HD), bf16),
            pltpu.VMEM((wide, HD), bf16),
            pltpu.VMEM((wide, HD), bf16),
            pltpu.VMEM((2 * HD, wide), bf16),
            pltpu.VMEM((2 * HD, wide), bf16),
            pltpu.VMEM((devices, BLOCK, wide), f32),
            pltpu.VMEM((devices, 1, wide), f32),
            pltpu.VMEM((HD + ONES, wide), f32),
            pltpu.VMEM((1, wide), f32),
            pltpu.VMEM((RING, 2, BLOCK, HD), f32),
            pltpu.VMEM((RING, 2, BLOCK, HD), bf16),
            pltpu.VMEM((RING, 2, BLOCK, HD), bf16),
            pltpu.VMEM((2, 4, 2, BLOCK, HD), bf16),
            pltpu.VMEM((2, 4, 2, BLOCK, HD), bf16),
            dma((2, 4, 4)),
            dma((2, 4, 4)),
            dma((RING, 4)),
            dma((RING, 4)),
            dma((RING,)),
            dma((RING,)),
            dma((2, 4, 2)),
            dma((2, 4, 2)),
        ],
        name="fused",
        compiler_params=pltpu.CompilerParams(collective_id=0, has_side_effects=True),
    )(ids, mask, queries, grads, keys, values)


def solution(mesh):
    def per_device(queries, key_rows, value_rows, out_grad, tile_ids, tile_mask):
        return fused(queries, out_grad, key_rows, value_rows, tile_ids, tile_mask)

    spec = P(("batch", "seq"), "head")
    return jax.shard_map(
        per_device,
        mesh=mesh,
        in_specs=(spec, spec, spec, spec, P("batch"), P("batch", None)),
        out_specs=(spec,) * 4,
        check_vma=False,
    )
```
